256 devices in a mesh: dp: 8 (over z), space: 32 (over x, y, core).
Axes of the slice: x: 4, y: 4, z: 8, core: 2. Of those that a mesh axis runs over, the one named last changes fastest.
Arguments:
- volume: bfloat16 [8, 32, 8, 16, 16, 256], P('dp', 'space'), may hold values from -6 to 6
- fine_filter: bfloat16 [3, 3, 3, 256, 256], P(None, None, None, 'dp'), may hold values from -0.078125 to 0.078125
- coarse_filter: bfloat16 [3, 3, 3, 256, 256], P(None, None, None, 'dp'), may hold values from -0.078125 to 0.078125
- fine_bias: float32 [256], replicated, may hold values from -3 to 3
- coarse_bias: float32 [256], replicated, may hold values from -3 to 3
Outputs:
- context: bfloat16 [8, 32, 8, 16, 16, 256], P('dp', 'space')
The draws below stay inside these ranges and needn't reach their ends.
All inputs are finite; a program needn't handle non-finite values.
Results may differ from the reference program's by a relative error of at most 0.0047.
Values may be sent and summed in bfloat16 or wider, within the bound.
No kernel may reach another device: no remote copies, remote signals or barrier semaphores. Data moves between devices by JAX's collectives and lax.ppermute only.
A program may use at most 128 MiB of HBM per device.

```python
import jax
import jax.numpy as jnp
from jax import lax

C = 256
X = 64
Y = 64
Z = 16
BX = 8
CROPS = 8
GX = 8
GY = 4
BY = 16
BRICKS = 32


def level_of(stream_key, shape, split, least, largest):
    factor_of, own = 1.0, jax.random.fold_in(stream_key, 6)
    for position, blocks in split:
        heights = jnp.exp(jax.random.uniform(jax.random.fold_in(own, position), (blocks,), jnp.float32, least / len(split), largest / len(split)))
        factor_of = factor_of * jnp.repeat(heights, shape[position] // blocks).reshape([-1 if axis == position else 1 for axis in range(len(shape))])
    return factor_of


def noise(rng, shape, scale, most, shards=(), held_as=jnp.bfloat16):
    factor_of = level_of(rng, shape, shards, -0.22, 0.18) if shards else 1.0
    array = jax.random.normal(rng, shape, jnp.float32) * scale * factor_of
    return jnp.minimum(jnp.maximum(array, -most), most).astype(held_as)


def setup_inputs(seed: int = 0) -> dict:
    streams_of = jax.random.split(jax.random.key(seed), 6)
    return {
        "volume": noise(streams_of[0], (CROPS, BRICKS, BX, BY, Z, C), 1.0, 6.0, ((0, 8), (1, 32))),
        "fine_filter": noise(streams_of[1], (3, 3, 3, C, C), (27 * C) ** -0.5, 0.078125, ((3, 8),)),
        "coarse_filter": noise(streams_of[2], (3, 3, 3, C, C), (27 * C) ** -0.5, 0.078125, ((3, 8),)),
        "fine_bias": noise(streams_of[3], (C,), 0.5, 3.0, (), jnp.float32),
        "coarse_bias": noise(streams_of[4], (C,), 0.5, 3.0, (), jnp.float32),
    }


def dilated(crop, filt, bias, rate):
    out = lax.conv_general_dilated(crop[None].astype(jnp.float32), filt.astype(jnp.float32), (1, 1, 1), [(rate, rate)] * 3, rhs_dilation=(rate, rate, rate), dimension_numbers=("NDHWC", "DHWIO", "NDHWC"), precision=lax.Precision.HIGHEST)[0]
    return (crop.astype(jnp.float32) + jax.nn.gelu(out + bias)).astype(jnp.bfloat16)


def reference(volume, fine_filter, coarse_filter, fine_bias, coarse_bias):
    crops = volume.reshape(CROPS, GX, GY, BX, BY, Z, C).transpose(0, 1, 3, 2, 4, 5, 6).reshape(CROPS, X, Y, Z, C)

    def one_crop(crop):
        middle = dilated(crop, fine_filter, fine_bias, 4)
        return dilated(middle, coarse_filter, coarse_bias, 8)

    result = lax.map(one_crop, crops)
    return result.reshape(CROPS, GX, BX, GY, BY, Z, C).transpose(0, 1, 3, 2, 4, 5, 6).reshape(CROPS, GX * GY, BX, BY, Z, C)
```

```python
import functools

import jax
import jax.numpy as jnp
from jax import lax
from jax.experimental import pallas as pl
from jax.experimental.pallas import tpu as pltpu
from jax.sharding import Mesh
from jax.sharding import PartitionSpec as P

C = 256
TAPS = 27
ROWS = TAPS * 32
HALF = ROWS // 2
COPIES = 16
PIECES = 18
VMEM = pl.BlockSpec(memory_space=pltpu.VMEM)
ANY = pl.BlockSpec(memory_space=pl.ANY)
SMEM = pl.BlockSpec(memory_space=pltpu.SMEM)


def one_hot(source):
    row = lax.broadcasted_iota(jnp.int32, (C, C), 0)
    column = lax.broadcasted_iota(jnp.int32, (C, C), 1)
    return jnp.where(column == source(row), 1.0, 0.0).astype(jnp.bfloat16)


def select(matrix, rows):
    return jnp.dot(matrix, rows, preferred_element_type=jnp.float32).astype(jnp.bfloat16)


def brick_row(r):
    py, pzh, pzl, zq, yq = r >> 6, (r >> 5) & 1, (r >> 4) & 1, (r >> 2) & 3, r & 3
    return (4 * yq + py) * 16 + 4 * zq + 2 * pzh + pzl


def brick_row_inverse(r):
    by, bz = r >> 4, r & 15
    return ((by & 3) << 6) + ((bz & 3) << 4) + ((bz >> 2) << 2) + (by >> 2)


def wire_row(r, shift):
    pzl, zq, xh, y = r >> 7, (r >> 5) & 3, (r >> 4) & 1, (r & 15) + shift
    found = ((y >> 2) << 6) + (xh << 5) + (pzl << 4) + (zq << 2) + (y & 3)
    return jnp.where((y >= 0) & (y < 16), found, -1)


def wire_row_inverse(r):
    j, xh, pzl, zq, yq = r >> 6, (r >> 5) & 1, (r >> 4) & 1, (r >> 2) & 3, r & 3
    return (pzl << 7) + (zq << 5) + (xh << 4) + (j << 2) + yq


def moved_row(r, shift):
    y = (r & 15) + shift
    return jnp.where((y >= 0) & (y < 16), r + shift, -1)


def all_of(copies):
    for copy in copies:
        copy.start()
    return copies


def stage_kernel(place, fine, coarse, message, held, sem):
    base = pl.multiple_of(place[1] * HALF, 16)
    parts = [pl.ds(n * HALF, HALF) for n in range(2)]
    loads = all_of(
        [
            pltpu.make_async_copy(rows.at[pl.ds(base, HALF)], held.at[part], sem.at[0, n])
            for n, (rows, part) in enumerate(zip((fine, coarse), parts))
        ]
    )
    stores = []
    for n, part in enumerate(parts):
        loads[n].wait()
        stores += all_of([pltpu.make_async_copy(held.at[part], message.at[part], sem.at[1, n])])
    for store in stores:
        store.wait()


def pack_kernel(brick, wire, held, packed, sem):
    loads = [pltpu.make_async_copy(brick.at[x], held.at[x], sem.at[0, x]) for x in range(8)]
    all_of([loads[x] for x in (0, 4, 1, 5, 2, 6, 3, 7)])
    order = one_hot(brick_row)
    stores = []
    for half in range(2):
        for x in (2 * half, 2 * half + 4, 2 * half + 1, 2 * half + 5):
            loads[x].wait()
        for px in (2 * half, 2 * half + 1):
            for xh in range(2):
                rows = select(order, held[px + 4 * xh])
                packed[px * 8 : px * 8 + 8, xh * 32 : xh * 32 + 32, :] = rows.reshape(8, 32, C)
        block = pl.ds(half * 16, 16)
        stores += all_of([pltpu.make_async_copy(packed.at[block], wire.at[block], sem.at[1, half])])
    for store in stores:
        store.wait()


def unpack_kernel(wire, brick, held, placed, sem):
    loads = all_of(
        [
            pltpu.make_async_copy(wire.at[pl.ds(px * 8, 8)], held.at[pl.ds(px * 8, 8)], sem.at[0, px])
            for px in range(4)
        ]
    )
    order = one_hot(brick_row_inverse)
    stores = []
    for half in range(2):
        loads[2 * half].wait()
        loads[2 * half + 1].wait()
        places = [(px, xh) for px in (2 * half, 2 * half + 1) for xh in range(2)]
        for px, xh in places:
            rows = held[px * 8 : px * 8 + 8, xh * 32 : xh * 32 + 32, :].reshape(C, C)
            placed[px + 4 * xh] = select(order, rows)
        for px, xh in places:
            x = px + 4 * xh
            stores += all_of([pltpu.make_async_copy(placed.at[x], brick.at[x], sem.at[1, x])])
    for store in stores:
        store.wait()


def weight_copies(place, own, moved, swapped, part, held, sem):
    k, core = place[0], place[1]
    copies = [(own, held.at[k])]
    for side, pieces in ((core, moved), (1 - core, swapped)):
        rows = pl.ds(pl.multiple_of(side * HALF, 16), HALF)
        for step in range(1, 4):
            for piece, owner in ((2 * step - 2, k - step + 8), (2 * step - 1, k + step)):
                source = pieces[piece].at[pl.ds(part * HALF, HALF)]
                copies.append((source, held.at[lax.rem(owner, 8), rows]))
        copies.append((pieces[6 + part], held.at[lax.rem(k + 4, 8), rows]))
    return [
        pltpu.make_async_copy(source, target, sem.at[n])
        for n, (source, target) in enumerate(copies)
    ]


def taps_of(shifted, held, step, tz_from_zi):
    left, right = [], []
    for tz, zi in tz_from_zi:
        for tx in range(3):
            for ty in range(3):
                slab = shifted[ty, :, zi, tx * step * 16 : tx * step * 16 + 256, :]
                left.append(slab.reshape(2 * 256, C))
                tap = (tx * 3 + ty) * 3 + tz
                right.append(held[:, tap * 32 : tap * 32 + 32, :].reshape(C, C))
    return jnp.dot(
        jnp.concatenate(left, axis=1),
        jnp.concatenate(right, axis=0),
        preferred_element_type=jnp.float32,
    )


def block_kernel(place, wire, fine_bias, coarse_bias, *rest):
    pieces = rest[:PIECES]
    out, received, near, far, fine, coarse, context, packed, sem = rest[PIECES:]
    loads = all_of(
        [
            pltpu.make_async_copy(
                wire.at[pl.ds(4 * i, 4)], received.at[pl.ds(4 * i, 4)], sem.at[0, i]
            )
            for i in range(8)
        ]
    )
    moved, swapped = pieces[2:10], pieces[10:]
    fine_copies = weight_copies(place, pieces[0], moved, swapped, 0, fine, sem.at[1])
    coarse_copies = weight_copies(place, pieces[1], moved, swapped, 1, coarse, sem.at[2])
    all_of(fine_copies)
    all_of(coarse_copies)
    zero = jnp.zeros((3, 2, 4, 32, C), jnp.bfloat16)
    near[:, :, :, 0:16, :] = zero[:, :, :, :16]
    near[:, :, :, 272:288, :] = zero[:, :, :, :16]
    far[:, :, :, 0:32, :] = zero
    far[:, :, :, 288:320, :] = zero
    for load in loads:
        load.wait()
    for ty in range(3):
        order = one_hot(functools.partial(wire_row, shift=ty - 1))
        for i in range(8):
            rows = select(order, received[4 * i : 4 * i + 4].reshape(C, C))
            near[ty, :, :, 16 + 32 * i : 48 + 32 * i, :] = rows.reshape(2, 4, 32, C)
    for copy in fine_copies:
        copy.wait()
    for zo in range(4):
        pairs = [(tz, zo + tz - 1) for tz in range(3) if 0 <= zo + tz - 1 < 4]
        total = taps_of(near, fine, 1, pairs)
        here = near[1, :, zo, 16:272, :].reshape(512, C).astype(jnp.float32)
        middle = (here + jax.nn.gelu(total + fine_bias[...])).astype(jnp.bfloat16)
        far[1, :, zo, 32:288, :] = middle.reshape(2, 256, C)
    for copy in coarse_copies:
        copy.wait()
    for ty in (0, 2):
        order = one_hot(functools.partial(moved_row, shift=2 * (ty - 1)))
        for pzl in range(2):
            for z in range(4):
                far[ty, pzl, z, 32:288, :] = select(order, far[1, pzl, z, 32:288, :])
    for zo in range(4):
        pairs = [(tz, zo + 2 * (tz - 1)) for tz in range(3) if 0 <= zo + 2 * (tz - 1) < 4]
        total = taps_of(far, coarse, 2, pairs)
        here = far[1, :, zo, 32:288, :].reshape(512, C).astype(jnp.float32)
        result = (here + jax.nn.gelu(total + coarse_bias[...])).astype(jnp.bfloat16)
        context[:, zo] = result.reshape(2, 256, C)
    order = one_hot(wire_row_inverse)
    for i in range(8):
        rows = select(order, context[:, :, 32 * i : 32 * i + 32, :].reshape(C, C))
        packed[4 * i : 4 * i + 4] = rows.reshape(4, 64, C)
    stores = all_of(
        [
            pltpu.make_async_copy(
                packed.at[pl.ds(4 * i, 4)], out.at[pl.ds(4 * i, 4)], sem.at[0, 8 + i]
            )
            for i in range(8)
        ]
    )
    for store in stores:
        store.wait()


def shift(value, by):
    return lax.ppermute(value, "dp", [(k, (k + by) % 8) for k in range(8)])


def swap(value):
    return lax.ppermute(value, "core", [(0, 1), (1, 0)])


def gather_filters(shards, place):
    own = [shard.reshape(ROWS, C) for shard in shards]
    message = pl.pallas_call(
        stage_kernel,
        out_shape=jax.ShapeDtypeStruct((ROWS, C), jnp.bfloat16),
        in_specs=[SMEM, ANY, ANY],
        out_specs=ANY,
        scratch_shapes=[pltpu.VMEM((ROWS, C), jnp.bfloat16), pltpu.SemaphoreType.DMA((2, 2))],
        name="stage",
    )(place, *own)
    forward = backward = message
    moved, swapped = [], []
    for step in range(1, 5):
        if step == 4:
            forward, backward = forward[:HALF], backward[HALF:]
        forward = shift(forward, 1)
        backward = shift(backward, -1)
        swapped.append(swap(forward))
        swapped.append(swap(backward))
        moved += [forward, backward]
    return (*own, *moved, *swapped)


def on_device(volume, fine_filter, coarse_filter, fine_bias, coarse_bias):
    brick = volume.reshape(8, 256, C)
    place = jnp.stack([lax.axis_index("dp"), lax.axis_index("core")]).astype(jnp.int32)
    wire_shape = jax.ShapeDtypeStruct((32, 64, C), jnp.bfloat16)

    pieces = gather_filters((fine_filter, coarse_filter), place)
    outgoing = pl.pallas_call(
        pack_kernel,
        out_shape=wire_shape,
        in_specs=[ANY],
        out_specs=ANY,
        scratch_shapes=[
            pltpu.VMEM((8, 256, C), jnp.bfloat16),
            pltpu.VMEM((32, 64, C), jnp.bfloat16),
            pltpu.SemaphoreType.DMA((2, 8)),
        ],
        name="pack",
    )(brick)
    received = lax.all_to_all(outgoing, ("x", "y", "core"), 0, 0, tiled=True)
    outgoing = pl.pallas_call(
        block_kernel,
        out_shape=wire_shape,
        in_specs=[SMEM, ANY, VMEM, VMEM] + [ANY] * PIECES,
        out_specs=ANY,
        scratch_shapes=[
            pltpu.VMEM((32, 64, C), jnp.bfloat16),
            pltpu.VMEM((3, 2, 4, 288, C), jnp.bfloat16),
            pltpu.VMEM((3, 2, 4, 320, C), jnp.bfloat16),
            pltpu.VMEM((8, ROWS, C), jnp.bfloat16),
            pltpu.VMEM((8, ROWS, C), jnp.bfloat16),
            pltpu.VMEM((2, 4, 256, C), jnp.bfloat16),
            pltpu.VMEM((32, 64, C), jnp.bfloat16),
            pltpu.SemaphoreType.DMA((3, COPIES)),
        ],
        name="block",
    )(place, received, fine_bias.reshape(1, C), coarse_bias.reshape(1, C), *pieces)
    received = lax.all_to_all(outgoing, ("x", "y", "core"), 0, 0, tiled=True)
    brick = pl.pallas_call(
        unpack_kernel,
        out_shape=jax.ShapeDtypeStruct((8, 256, C), jnp.bfloat16),
        in_specs=[ANY],
        out_specs=ANY,
        scratch_shapes=[
            pltpu.VMEM((32, 64, C), jnp.bfloat16),
            pltpu.VMEM((8, 256, C), jnp.bfloat16),
            pltpu.SemaphoreType.DMA((2, 8)),
        ],
        name="unpack",
    )(received)
    return brick.reshape(volume.shape)


def solution(mesh):
    grid = Mesh(mesh.devices.reshape(8, 4, 4, 2), ("dp", "x", "y", "core"))
    space = ("x", "y", "core")
    return jax.shard_map(
        on_device,
        mesh=grid,
        in_specs=(
            P("dp", space, None, None, None, None),
            P(None, None, None, "dp", None),
            P(None, None, None, "dp", None),
            P(),
            P(),
        ),
        out_specs=P("dp", space, None, None, None, None),
        check_vma=False,
    )
```

```python
import functools

import jax
import jax.numpy as jnp
from jax import lax
from jax.experimental import pallas as pl
from jax.experimental.pallas import tpu as pltpu
from jax.sharding import Mesh
from jax.sharding import PartitionSpec as P

C = 256
TAPS = 27
ROWS = TAPS * 32
HALF = ROWS // 2
PIECES = 18
PART = 48
VMEM = pl.BlockSpec(memory_space=pltpu.VMEM)
ANY = pl.BlockSpec(memory_space=pl.ANY)


def one_hot(source):
    row = lax.broadcasted_iota(jnp.int32, (C, C), 0)
    column = lax.broadcasted_iota(jnp.int32, (C, C), 1)
    return jnp.where(column == source(row), 1.0, 0.0).astype(jnp.bfloat16)


def select(matrix, rows):
    return jnp.dot(matrix, rows, preferred_element_type=jnp.float32).astype(jnp.bfloat16)


def brick_row(r):
    py, pzh, pzl, zq, yq = r >> 6, (r >> 5) & 1, (r >> 4) & 1, (r >> 2) & 3, r & 3
    return (4 * yq + py) * 16 + 4 * zq + 2 * pzh + pzl


def brick_row_inverse(r):
    by, bz = r >> 4, r & 15
    return ((by & 3) << 6) + ((bz & 3) << 4) + ((bz >> 2) << 2) + (by >> 2)


def wire_row(r, shift):
    pzl, zq, xh, y = r >> 7, (r >> 5) & 3, (r >> 4) & 1, (r & 15) + shift
    found = ((y >> 2) << 6) + (xh << 5) + (pzl << 4) + (zq << 2) + (y & 3)
    return jnp.where((y >= 0) & (y < 16), found, -1)


def wire_row_inverse(r):
    j, xh, pzl, zq, yq = r >> 6, (r >> 5) & 1, (r >> 4) & 1, (r >> 2) & 3, r & 3
    return (pzl << 7) + (zq << 5) + (xh << 4) + (j << 2) + yq


def moved_row(r, shift):
    y = (r & 15) + shift
    return jnp.where((y >= 0) & (y < 16), r + shift, -1)


def in_parts(source, target, sem, parts):
    size = source.shape[0] // parts
    for n in range(parts):
        part = pl.ds(n * size, size)
        pltpu.make_async_copy(source.at[part], target.at[part], sem).start()
    return pltpu.make_async_copy(source, target, sem)


def pack_kernel(brick, wire, held, packed, sem):
    loads = {x: in_parts(brick.at[x], held.at[x], sem.at[0, x], 4) for x in (0, 4, 1, 5, 2, 6, 3, 7)}
    order = one_hot(brick_row)
    stores = []
    for half in range(2):
        for x in (2 * half, 2 * half + 4, 2 * half + 1, 2 * half + 5):
            loads[x].wait()
        for px in (2 * half, 2 * half + 1):
            for xh in range(2):
                rows = select(order, held[px + 4 * xh])
                packed[px * 8 : px * 8 + 8, xh * 32 : xh * 32 + 32, :] = rows.reshape(8, 32, C)
        block = pl.ds(half * 16, 16)
        stores.append(in_parts(packed.at[block], wire.at[block], sem.at[1, half], 16))
    for store in stores:
        store.wait()


def unpack_kernel(wire, brick, placed, sem):
    order = one_hot(brick_row_inverse)
    stores = []
    for half in range(2):
        places = [(px, xh) for px in (2 * half, 2 * half + 1) for xh in range(2)]
        for px, xh in places:
            rows = wire[px * 8 : px * 8 + 8, xh * 32 : xh * 32 + 32, :].reshape(C, C)
            placed[px + 4 * xh] = select(order, rows)
        for px, xh in places:
            x = px + 4 * xh
            stores.append(in_parts(placed.at[x], brick.at[x], sem.at[x], 4))
    for store in stores:
        store.wait()


def start_weights(own, moved, swapped, held, sem):
    k, core = lax.axis_index("dp"), lax.axis_index("core")

    def lay(pieces, n):
        targets = [(k, 0)]
        for step in range(1, 4):
            for owner in (k - step + 8, k + step):
                targets.append((lax.rem(owner, 8), 0))
        targets += [(lax.rem(k + 4, 8), 0), (lax.rem(k + 4, 8), HALF)]
        for m, (piece, (slot, base)) in enumerate(zip((own[n], *pieces), targets)):
            for first in range(0, piece.shape[0], PART):
                source = piece.at[pl.ds(first, PART)]
                target = held.at[n, slot, pl.ds(base + first, PART)]
                pltpu.make_async_copy(source, target, sem.at[n, m]).start()

    @pl.when(core == 0)
    def _():
        lay(moved, 0)
        lay(swapped, 1)

    @pl.when(core != 0)
    def _():
        lay(swapped, 0)
        lay(moved, 1)


def arrivals(part, own, moved, held, sem):
    return [
        pltpu.make_async_copy(piece, held.at[part, 0, pl.ds(0, piece.shape[0])], sem.at[part, n])
        for n, piece in enumerate((own[part], *moved))
    ]


def taps_of(shifted, held, step, tz_from_zi):
    left, right = [], []
    for tz, zi in tz_from_zi:
        for tx in range(3):
            for ty in range(3):
                slab = shifted[ty, :, zi, tx * step * 16 : tx * step * 16 + 256, :]
                left.append(slab.reshape(2 * 256, C))
                tap = (tx * 3 + ty) * 3 + tz
                right.append(held[:, tap * 32 : tap * 32 + 32, :].reshape(C, C))
    return jnp.dot(
        jnp.concatenate(left, axis=1),
        jnp.concatenate(right, axis=0),
        preferred_element_type=jnp.float32,
    )


def block_kernel(wire, fine_bias, coarse_bias, *rest):
    pieces = rest[:PIECES]
    out, received, near, far, held, context, packed, sem, weight_sem = rest[PIECES:]
    load = in_parts(wire, received, sem.at[0], 32)
    moved, swapped = pieces[2:10], pieces[10:]
    own = pieces[:2]
    start_weights(own, moved, swapped, held, weight_sem)
    zero = jnp.zeros((3, 2, 4, 32, C), jnp.bfloat16)
    near[:, :, :, 0:16, :] = zero[:, :, :, :16]
    near[:, :, :, 272:288, :] = zero[:, :, :, :16]
    far[:, :, :, 0:32, :] = zero
    far[:, :, :, 288:320, :] = zero
    load.wait()
    for ty in range(3):
        order = one_hot(functools.partial(wire_row, shift=ty - 1))
        for i in range(8):
            rows = select(order, received[4 * i : 4 * i + 4].reshape(C, C))
            near[ty, :, :, 16 + 32 * i : 48 + 32 * i, :] = rows.reshape(2, 4, 32, C)
    for arrival in arrivals(0, own, moved, held, weight_sem):
        arrival.wait()
    for zo in range(4):
        pairs = [(tz, zo + tz - 1) for tz in range(3) if 0 <= zo + tz - 1 < 4]
        total = taps_of(near, held.at[0], 1, pairs)
        here = near[1, :, zo, 16:272, :].reshape(512, C).astype(jnp.float32)
        middle = (here + jax.nn.gelu(total + fine_bias[...])).astype(jnp.bfloat16)
        far[1, :, zo, 32:288, :] = middle.reshape(2, 256, C)
    for arrival in arrivals(1, own, moved, held, weight_sem):
        arrival.wait()
    for ty in (0, 2):
        order = one_hot(functools.partial(moved_row, shift=2 * (ty - 1)))
        for pzl in range(2):
            for z in range(4):
                far[ty, pzl, z, 32:288, :] = select(order, far[1, pzl, z, 32:288, :])
    for zo in range(4):
        pairs = [(tz, zo + 2 * (tz - 1)) for tz in range(3) if 0 <= zo + 2 * (tz - 1) < 4]
        total = taps_of(far, held.at[1], 2, pairs)
        here = far[1, :, zo, 32:288, :].reshape(512, C).astype(jnp.float32)
        result = (here + jax.nn.gelu(total + coarse_bias[...])).astype(jnp.bfloat16)
        context[:, zo] = result.reshape(2, 256, C)
    order = one_hot(wire_row_inverse)
    stores = []
    for half in range(2):
        for i in range(4 * half, 4 * half + 4):
            rows = select(order, context[:, :, 32 * i : 32 * i + 32, :].reshape(C, C))
            packed[4 * i : 4 * i + 4] = rows.reshape(4, 64, C)
        block = pl.ds(16 * half, 16)
        stores.append(in_parts(packed.at[block], out.at[block], sem.at[1 + half], 16))
    for store in stores:
        store.wait()


def shift(value, by):
    return lax.ppermute(value, "dp", [(k, (k + by) % 8) for k in range(8)])


def swap(value):
    return lax.ppermute(value, "core", [(0, 1), (1, 0)])


def gather_filters(shards):
    own = [shard.reshape(ROWS, C) for shard in shards]
    message = jnp.where(lax.axis_index("core") == 0, *own)
    forward = backward = message
    moved, swapped = [], []
    for step in range(1, 5):
        if step == 4:
            forward, backward = forward[:HALF], backward[HALF:]
        forward = shift(forward, 1)
        backward = shift(backward, -1)
        swapped.append(swap(forward))
        swapped.append(swap(backward))
        moved += [forward, backward]
    return (*own, *moved, *swapped)


def on_device(volume, fine_filter, coarse_filter, fine_bias, coarse_bias):
    brick = volume.reshape(8, 256, C)
    wire_shape = jax.ShapeDtypeStruct((32, 64, C), jnp.bfloat16)

    pieces = gather_filters((fine_filter, coarse_filter))
    outgoing = pl.pallas_call(
        pack_kernel,
        out_shape=wire_shape,
        in_specs=[ANY],
        out_specs=ANY,
        scratch_shapes=[
            pltpu.VMEM((8, 256, C), jnp.bfloat16),
            pltpu.VMEM((32, 64, C), jnp.bfloat16),
            pltpu.SemaphoreType.DMA((2, 8)),
        ],
        name="pack",
    )(brick)
    received = lax.all_to_all(outgoing, ("x", "y", "core"), 0, 0, tiled=True)
    outgoing = pl.pallas_call(
        block_kernel,
        out_shape=wire_shape,
        in_specs=[ANY, VMEM, VMEM] + [ANY] * PIECES,
        out_specs=ANY,
        scratch_shapes=[
            pltpu.VMEM((32, 64, C), jnp.bfloat16),
            pltpu.VMEM((3, 2, 4, 288, C), jnp.bfloat16),
            pltpu.VMEM((3, 2, 4, 320, C), jnp.bfloat16),
            pltpu.VMEM((2, 8, ROWS, C), jnp.bfloat16),
            pltpu.VMEM((2, 4, 256, C), jnp.bfloat16),
            pltpu.VMEM((32, 64, C), jnp.bfloat16),
            pltpu.SemaphoreType.DMA((16,)),
            pltpu.SemaphoreType.DMA((2, 9)),
        ],
        name="block",
    )(received, fine_bias.reshape(1, C), coarse_bias.reshape(1, C), *pieces)
    received = lax.all_to_all(outgoing, ("x", "y", "core"), 0, 0, tiled=True)
    brick = pl.pallas_call(
        unpack_kernel,
        out_shape=jax.ShapeDtypeStruct((8, 256, C), jnp.bfloat16),
        in_specs=[VMEM],
        out_specs=ANY,
        scratch_shapes=[pltpu.VMEM((8, 256, C), jnp.bfloat16), pltpu.SemaphoreType.DMA((8,))],
        compiler_params=pltpu.CompilerParams(vmem_limit_bytes=6 << 20),
        name="unpack",
    )(received)
    return brick.reshape(volume.shape)


def solution(mesh):
    grid = Mesh(mesh.devices.reshape(8, 4, 4, 2), ("dp", "x", "y", "core"))
    space = ("x", "y", "core")
    return jax.shard_map(
        on_device,
        mesh=grid,
        in_specs=(
            P("dp", space, None, None, None, None),
            P(None, None, None, "dp", None),
            P(None, None, None, "dp", None),
            P(),
            P(),
        ),
        out_specs=P("dp", space, None, None, None, None),
        check_vma=False,
    )
```
